32 devices in a mesh: groups: 2 (over x), level: 16 (over z, y, core).
Axes of the slice: x: 2, y: 2, z: 4, core: 2. Of those that a mesh axis runs over, the one named last changes fastest.
Arguments:
- latents: bfloat16 [64, 256, 640], P(('groups', 'level')), parts along dimension 0, may hold values from -6 to 6
- levels: int32 [64], P(('groups', 'level')), parts along dimension 0, may hold values from 0 to 15
- back_reach: int32 [64], P(('groups', 'level')), parts along dimension 0, may hold values from 1 to 2
- text_ids: int32 [154], P('groups'), parts along dimension 0, may hold values from 0 to 49407
- text_table: bfloat16 [49408, 1024], P('level'), may hold values from -6 to 6
- text_proj: bfloat16 [1024, 640], replicated, may hold values from -0.75 to 0.75
- level_embed: float32 [16, 640], replicated, may hold values from -3 to 3
- step_rate: float32 [16], replicated, may hold values from 0.3 to 1
- norm_gain: float32 [640], replicated, may hold values from 0.5 to 1.5
- w_query: bfloat16 [640, 640], replicated
- w_key: bfloat16 [640, 640], replicated
- w_value: bfloat16 [640, 640], replicated, may hold values from -0.25 to 0.25
- w_out: bfloat16 [640, 640], replicated, may hold values from -0.25 to 0.25
Outputs:
- queue_out: bfloat16 [64, 256, 640], P(('groups', 'level')), parts along dimension 0
The draws below stay inside these ranges and needn't reach their ends.
There are 2 independent parts, one for each index of `groups`. The reference program is written for one: setup_inputs(seed, part) draws one part's arguments, and reference() takes and returns one part's arrays. A program takes and returns all parts, laid end to end along the dimension named above; an argument that names none is the same for every part. Nothing has to cross between parts.
All inputs are finite; a program needn't handle non-finite values.
Results may differ from the reference program's by a relative error of at most 0.007.
Values may be sent and summed in bfloat16 or wider, within the bound.
A program may use at most 64 MiB of HBM per device.

```python
import math
import jax
import jax.numpy as jnp
import numpy as np
from jax import lax

C = 640
DH = 64
P_SIZE = 256
F_DEV = 2
BAND = 2
LEVELS = 16
STEPS = 3
VOCAB = 49408
CTXW = 1024
NTEXT = 77
FRAMES = 32


def query_key_pair(key):
    base = jax.random.normal(jax.random.fold_in(key, 7), (C, C), jnp.float32) / math.sqrt(C)
    other = jax.random.normal(jax.random.fold_in(key, 11), (C, C), jnp.float32) / math.sqrt(C)
    first = base
    second = other
    return (first, second)


def draw_w_query(key, part):
    return query_key_pair(key)[0].astype(jnp.bfloat16)


def draw_w_key(key, part):
    return query_key_pair(key)[1].astype(jnp.bfloat16)


def touch_ends(result, stream_key, low, high):
    shape = result.shape
    spot = [jax.random.randint(jax.random.fold_in(stream_key, axis), (), 0, shape[axis]) for axis in range(len(shape))]
    result = result.at[tuple(spot)].set(low)
    longest = shape.index(max(shape))
    spot[longest] = (spot[longest] + 1) % shape[longest]
    return result.at[tuple(spot)].set(high)


def steps_of(stream_key, dims, pieces, smallest, largest):
    loudness, own = 1.0, jax.random.fold_in(stream_key, 6)
    for dim, parts in pieces:
        draws = jnp.exp(jax.random.uniform(jax.random.fold_in(own, dim), (parts,), jnp.float32, smallest / len(pieces), largest / len(pieces)))
        loudness = loudness * jnp.repeat(draws, dims[dim] // parts).reshape([-1 if axis == dim else 1 for axis in range(len(dims))])
    return loudness


def rank_table(amount, slope):
    loads = [(1 << 20) // math.isqrt(standing ** slope) + 1 for standing in range(1, amount + 1)]
    width = 1 + sum(loads) // (1 << 30)
    return np.cumsum(np.array([max(1, weight // width) for weight in loads]))


def ranked(rng, shape, number_of, lean):
    grid = rank_table(number_of, lean)
    lot = jax.random.randint(jax.random.fold_in(rng, 1), shape, 0, int(grid[number_of - 1]))
    standing = jnp.searchsorted(jnp.asarray(grid, jnp.int32), lot, side="right")
    return jax.random.permutation(jax.random.fold_in(rng, 2), number_of)[standing].astype(jnp.int32)


def noise(stream_key, extent, width, most, shards=(), kind=jnp.bfloat16):
    result = width * jax.random.normal(stream_key, extent, jnp.float32)
    if shards:
        result = result * steps_of(stream_key, extent, shards, -0.22, 0.18)
    return jnp.clip(result, -most, most).astype(kind)


def setup_inputs(seed: int = 0, part: int = 0) -> dict:
    arg_keys = jax.random.split(jax.random.key(seed), 14)
    own_keys = jax.random.split(jax.random.fold_in(arg_keys[13], part), 14)
    latents = noise(own_keys[0], (FRAMES, P_SIZE, C), 1.0, 6.0, ((0, 16),))
    levels = touch_ends(jax.random.randint(own_keys[1], (FRAMES,), 0, LEVELS), jax.random.fold_in(own_keys[1], 1), 0, LEVELS - 1).astype(jnp.int32)
    back_reach = touch_ends(jax.random.randint(own_keys[2], (FRAMES,), 1, BAND + 1), jax.random.fold_in(own_keys[2], 1), 1, BAND).astype(jnp.int32)
    text_ids = touch_ends(ranked(own_keys[3], (NTEXT,), VOCAB, 2), jax.random.fold_in(own_keys[3], 3), 0, VOCAB - 1).astype(jnp.int32)
    text_table = noise(arg_keys[4], (VOCAB, CTXW), 1.0, 6.0, ((0, 16),))
    text_proj = noise(arg_keys[5], (CTXW, C), (CTXW // 16) ** -0.5, 0.75)
    level_embed = noise(arg_keys[6], (LEVELS, C), 0.5, 3.0, (), jnp.float32)
    step_rate = jnp.clip(jnp.exp(jax.random.uniform(arg_keys[7], (LEVELS,), jnp.float32, math.log(0.3), math.log(1.0))), 0.3, 1.0)
    norm_gain = jnp.clip(1.0 + 0.1 * jax.random.normal(arg_keys[8], (C,), jnp.float32), 0.5, 1.5)
    w_query = draw_w_query(jax.random.fold_in(arg_keys[13], 71), part)
    w_key = draw_w_key(jax.random.fold_in(arg_keys[13], 71), part)
    w_value = noise(arg_keys[11], (C, C), C ** -0.5, 0.25)
    w_out = noise(arg_keys[12], (C, C), C ** -0.5, 0.25)
    return {"latents": latents, "levels": levels, "back_reach": back_reach, "text_ids": text_ids, "text_table": text_table, "text_proj": text_proj, "level_embed": level_embed, "step_rate": step_rate, "norm_gain": norm_gain, "w_query": w_query, "w_key": w_key, "w_value": w_value, "w_out": w_out}


def reference(latents, levels, back_reach, text_ids, text_table, text_proj, level_embed, step_rate, norm_gain, w_query, w_key, w_value, w_out):
    pooled = lax.optimization_barrier(jnp.mean(text_table[text_ids].astype(jnp.float32), axis=0))
    text_vec = jnp.dot(pooled.astype(jnp.bfloat16)[None, :], text_proj, preferred_element_type=jnp.float32)[0]
    cond = level_embed[levels] + text_vec[None, :]
    rate = step_rate[levels]
    frames = latents.shape[0]
    heads = C // DH
    frame_index = jnp.arange(frames, dtype=jnp.int32)
    scale = 1.0 / DH ** 0.5
    current = latents
    for step in range(STEPS):
        hin = current.astype(jnp.float32) + cond[:, None, :]
        normed = (hin * lax.rsqrt(lax.optimization_barrier(jnp.mean(hin * hin, axis=-1, keepdims=True)) + 1e-06) * norm_gain).astype(jnp.bfloat16)
        flat = normed.reshape(-1, C)
        query = jnp.dot(flat, w_query, preferred_element_type=jnp.float32).astype(jnp.bfloat16).reshape(frames, P_SIZE, heads, DH)
        keys = jnp.dot(flat, w_key, preferred_element_type=jnp.float32).astype(jnp.bfloat16).reshape(frames, P_SIZE, heads, DH)
        values = jnp.dot(flat, w_value, preferred_element_type=jnp.float32).astype(jnp.bfloat16).reshape(frames, P_SIZE, heads, DH)
        pad_keys = jnp.pad(keys, ((BAND, BAND), (0, 0), (0, 0), (0, 0)))
        pad_values = jnp.pad(values, ((BAND, BAND), (0, 0), (0, 0), (0, 0)))
        query_f = query.astype(jnp.float32)
        score_list = []
        valid_list = []
        for offset in range(-BAND, BAND + 1):
            shifted = pad_keys[BAND + offset:BAND + offset + frames].astype(jnp.float32)
            raw = jnp.einsum('fphd,fphd->fph', query_f, shifted) * scale
            valid = (offset >= -back_reach) & (frame_index + offset >= 0) & (frame_index + offset < frames)
            score_list.append(jnp.where(valid[:, None, None], raw, -1e+30))
            valid_list.append(valid.astype(jnp.float32)[:, None, None])
        scores = jnp.stack(score_list)
        masks = jnp.stack(valid_list)
        top = lax.optimization_barrier(jnp.max(scores, axis=0))
        expo = jnp.exp(scores - top[None]) * masks
        weights = (expo / lax.optimization_barrier(jnp.sum(expo, axis=0))[None]).astype(jnp.bfloat16)
        attended = jnp.zeros((frames, P_SIZE, heads, DH), jnp.float32)
        for slot, offset in enumerate(range(-BAND, BAND + 1)):
            shifted = pad_values[BAND + offset:BAND + offset + frames].astype(jnp.float32)
            attended = attended + weights[slot].astype(jnp.float32)[..., None] * shifted
        attended = attended.astype(jnp.bfloat16).reshape(-1, C)
        noise_pred = jnp.dot(attended, w_out, preferred_element_type=jnp.float32).reshape(frames, P_SIZE, C)
        updated = (current.astype(jnp.float32) - rate[:, None, None] * noise_pred).astype(jnp.bfloat16)
        current = jnp.roll(updated, F_DEV, axis=0)
    return current
```

```python
import functools

import jax
import jax.numpy as jnp
from jax import lax
from jax.experimental import pallas as pl
from jax.experimental.pallas import tpu as pltpu
from jax.sharding import PartitionSpec as P

DH = 64
BAND = 2
STEPS = 3
SPAN = 2 * BAND + 1
MESH = pl.DeviceIdType.MESH


def queue_kernel(
    n,
    group,
    tokens_text,
    x_hbm,
    meta_ref,
    ids_ref,
    table_hbm,
    proj_hbm,
    embed_ref,
    srate_ref,
    gain_ref,
    wq_hbm,
    wk_hbm,
    wv_hbm,
    wo_hbm,
    out_hbm,
    recv,
    xa,
    xb,
    xo,
    normed,
    q_s,
    k_s,
    v_s,
    att_s,
    table,
    proj,
    wq,
    wk,
    wv,
    wo,
    pool,
    metas,
    cond,
    rate,
    mask,
    fold,
    unfold,
    x_send,
    x_recv,
    p_send,
    p_recv,
    m_send,
    m_recv,
    o_send,
    o_recv,
    local,
):
    me = lax.axis_index("level")
    fdev = x_hbm.shape[0]
    frames, pos, width = recv.shape
    barrier = pltpu.get_barrier_semaphore()
    for hop in range(1, n):
        pl.semaphore_signal(
            barrier, inc=1, device_id={"level": lax.rem(me + hop, n)}, device_id_type=MESH
        )
    stage = [
        pltpu.make_async_copy(src, dst, local.at[slot])
        for slot, (src, dst) in enumerate(
            (
                (table_hbm, table),
                (proj_hbm, proj),
                (wq_hbm, wq),
                (wk_hbm, wk),
                (wv_hbm, wv),
                (wo_hbm, wo),
                (x_hbm.at[:, me], recv.at[pl.ds(me * fdev, fdev)]),
                (meta_ref, metas.at[me]),
            )
        )
    ]
    for copy in stage:
        copy.start()
    pl.semaphore_wait(barrier, n - 1)

    def x_copy(peer, owner):
        return pltpu.make_async_remote_copy(
            src_ref=x_hbm.at[:, peer],
            dst_ref=recv.at[pl.ds(owner * fdev, fdev)],
            send_sem=x_send.at[peer],
            recv_sem=x_recv.at[owner],
            device_id={"level": peer},
            device_id_type=MESH,
        )

    def p_copy(peer, owner):
        return pltpu.make_async_remote_copy(
            src_ref=pool.at[owner],
            dst_ref=pool.at[owner],
            send_sem=p_send.at[peer],
            recv_sem=p_recv.at[owner],
            device_id={"level": peer},
            device_id_type=MESH,
        )

    def m_copy(peer, owner):
        return pltpu.make_async_remote_copy(
            src_ref=meta_ref,
            dst_ref=metas.at[owner],
            send_sem=m_send.at[peer],
            recv_sem=m_recv.at[owner],
            device_id={"level": peer},
            device_id_type=MESH,
        )

    peers = [lax.rem(me + hop, n) for hop in range(1, n)]
    for peer in peers:
        m_copy(peer, me).start()
    half = (n - 1) // 2
    for peer in peers[:half]:
        x_copy(peer, me).start()

    vocab = table.shape[0]
    own = ids_ref[...] - me * vocab
    hits = lax.broadcasted_iota(jnp.int32, (tokens_text, vocab), 1) == own
    counts = jnp.sum(hits.astype(jnp.float32), axis=0, keepdims=True)
    counts = jnp.broadcast_to(counts, (16, vocab)).astype(jnp.bfloat16)
    stage[0].wait()
    partial = jnp.dot(counts, table[...], preferred_element_type=jnp.float32)
    pool[me] = partial[0:1]
    for peer in peers:
        p_copy(peer, me).start()
    for peer in peers[half:]:
        x_copy(peer, me).start()

    heads = width // DH
    row = lax.broadcasted_iota(jnp.int32, (width, 128), 0)
    col = lax.broadcasted_iota(jnp.int32, (width, 128), 1) * DH
    fold[...] = ((row >= col) & (row < col + DH)).astype(jnp.float32).astype(jnp.bfloat16)
    row = lax.broadcasted_iota(jnp.int32, (128, width), 0) * DH
    col = lax.broadcasted_iota(jnp.int32, (128, width), 1)
    unfold[...] = ((col >= row) & (col < row + DH)).astype(jnp.float32).astype(jnp.bfloat16)
    edge = jnp.zeros((BAND, pos, width), jnp.bfloat16)
    for buffer in (k_s, v_s):
        buffer[0:BAND] = edge
        buffer[frames + BAND : frames + 2 * BAND] = edge

    stage[7].wait()
    for peer in peers:
        m_copy(peer, peer).wait_recv()
    facts = metas[...].reshape(n, 128)
    slot_index = lax.broadcasted_iota(jnp.int32, (n, 128), 0)
    bases = []
    for f in range(fdev):
        level = facts[:, f : f + 1]
        base = jnp.zeros((n, width), jnp.float32)
        speed = jnp.zeros((n, width), jnp.float32)
        for number in range(embed_ref.shape[0]):
            chosen = level == float(number)
            base = base + jnp.where(chosen, embed_ref[number : number + 1, :], 0.0)
            speed = speed + jnp.where(chosen, srate_ref[0:1, number : number + 1], 0.0)
        bases.append(base)
        reach = jnp.broadcast_to(facts[:, fdev + f : fdev + f + 1], (n, 128))
        spot = slot_index * fdev + f
        for s in range(n):
            rate[s * fdev + f] = speed[s : s + 1]
        for slot in range(SPAN):
            offset = slot - BAND
            valid = (
                (reach >= float(-offset)) & (spot + offset >= 0) & (spot + offset < frames)
            ).astype(jnp.float32)
            for s in range(n):
                mask[slot, s * fdev + f] = valid[s : s + 1]

    stage[1].wait()
    for peer in peers:
        p_copy(peer, peer).wait_recv()
    pooled = jnp.sum(pool[...], axis=0) / float(tokens_text)
    pooled = jnp.broadcast_to(pooled, (16, pooled.shape[1])).astype(jnp.bfloat16)
    text = jnp.dot(pooled, proj[...], preferred_element_type=jnp.float32)[0:1]
    for f in range(fdev):
        full = bases[f] + text
        for s in range(n):
            cond[s * fdev + f] = full[s : s + 1]

    for slot in (2, 3, 4, 5, 6):
        stage[slot].wait()
    for peer in peers:
        x_copy(peer, peer).wait_recv()

    rows = group * pos
    gain = gain_ref[...].reshape(1, 1, width)

    def project(source):
        def body(index, carry):
            at = pl.ds(index * group, group)
            hin = source[at].astype(jnp.float32) + cond[at]
            power = jnp.mean(hin * hin, axis=-1, keepdims=True)
            flat = (hin * lax.rsqrt(power + 1e-06) * gain).astype(jnp.bfloat16).reshape(rows, width)
            there = pl.ds(index * group + BAND, group)
            for weight, target, spot in ((wq, q_s, at), (wk, k_s, there), (wv, v_s, there)):
                target[spot] = (
                    jnp.dot(flat, weight[...], preferred_element_type=jnp.float32)
                    .astype(jnp.bfloat16)
                    .reshape(group, pos, width)
                )
            return carry

        lax.fori_loop(0, frames // group, body, 0)

    def attend(source, target, lead):
        scale = 1.0 / DH**0.5

        def body(index, carry):
            first = index * group
            at = pl.ds(first, group)
            query = q_s[at].reshape(rows, width)
            scores = []
            masks = []
            for slot in range(SPAN):
                keys = k_s[pl.ds(first + slot, group)].reshape(rows, width)
                raw = jnp.dot(query * keys, fold[...], preferred_element_type=jnp.float32) * scale
                valid = mask[slot, at]
                raw = jnp.where(valid > 0.0, raw.reshape(group, pos, 128), -1e30)
                scores.append(raw)
                masks.append(valid)
            top = functools.reduce(jnp.maximum, scores)
            expo = [jnp.exp(score - top) * valid for score, valid in zip(scores, masks)]
            inverse = 1.0 / functools.reduce(jnp.add, expo)
            total = None
            for slot in range(SPAN):
                weight = (expo[slot] * inverse).astype(jnp.bfloat16).reshape(rows, 128)
                spread = jnp.dot(weight, unfold[...], preferred_element_type=jnp.float32)
                values = v_s[pl.ds(first + slot, group)].reshape(rows, width)
                term = spread * values.astype(jnp.float32)
                total = term if total is None else total + term
            noise = jnp.dot(
                total.astype(jnp.bfloat16), wo[...], preferred_element_type=jnp.float32
            ).reshape(group, pos, width)
            fresh = source[at].astype(jnp.float32) - rate[at] * noise
            target[pl.ds(first + lead, group)] = fresh.astype(jnp.bfloat16)
            return carry

        lax.fori_loop(0, frames // group, body, 0)

    buffers = (recv, xa, xb, xo)
    for step in range(STEPS):
        source, target = buffers[step], buffers[step + 1]
        last = step == STEPS - 1
        project(source)
        attend(source, target, 0 if last else fdev)
        if not last:
            target[0:fdev] = target[frames : frames + fdev]

    def o_copy(section, owner, peer):
        return pltpu.make_async_remote_copy(
            src_ref=xo.at[pl.ds(section * fdev, fdev)],
            dst_ref=out_hbm.at[:, owner],
            send_sem=o_send.at[peer],
            recv_sem=o_recv.at[owner],
            device_id={"level": peer},
            device_id_type=MESH,
        )

    for peer in peers:
        o_copy(lax.rem(peer + n - 1, n), me, peer).start()
    keep = pltpu.make_async_copy(
        xo.at[pl.ds(lax.rem(me + n - 1, n) * fdev, fdev)], out_hbm.at[:, me], local.at[8]
    )
    keep.start()
    keep.wait()
    for peer in peers:
        x_copy(peer, me).wait_send()
        m_copy(peer, me).wait_send()
        p_copy(peer, me).wait_send()
    for peer in peers:
        o_copy(lax.rem(peer + n - 1, n), me, peer).wait_send()
        o_copy(lax.rem(me + n - 1, n), peer, me).wait_recv()


def fused(
    latents,
    levels,
    back_reach,
    text_ids,
    text_table,
    text_proj,
    level_embed,
    step_rate,
    norm_gain,
    w_query,
    w_key,
    w_value,
    w_out,
):
    n = lax.axis_size("level")
    fdev, tokens, width = latents.shape
    pos = tokens // n
    frames = fdev * n
    group = frames // 2
    bf16, f32 = jnp.bfloat16, jnp.float32
    meta = jnp.concatenate([levels, back_reach]).astype(f32)
    meta = jnp.pad(meta, (0, 128 - 2 * fdev))[None, :]
    srate = jnp.pad(step_rate, (0, 128 - step_rate.shape[0]))[None, :]
    anywhere = pl.BlockSpec(memory_space=pl.ANY)
    vmem = pl.BlockSpec(memory_space=pltpu.VMEM)
    dma = pltpu.SemaphoreType.DMA
    block = (frames, pos, width)
    out = pl.pallas_call(
        functools.partial(queue_kernel, n, group, text_ids.shape[0]),
        out_shape=jax.ShapeDtypeStruct((fdev, n, pos, width), bf16),
        in_specs=[
            anywhere,
            vmem,
            vmem,
            anywhere,
            anywhere,
            vmem,
            vmem,
            vmem,
            anywhere,
            anywhere,
            anywhere,
            anywhere,
        ],
        out_specs=anywhere,
        scratch_shapes=[
            pltpu.VMEM(block, bf16),
            pltpu.VMEM((frames + fdev, pos, width), bf16),
            pltpu.VMEM((frames + fdev, pos, width), bf16),
            pltpu.VMEM(block, bf16),
            pltpu.VMEM((8, 128), bf16),
            pltpu.VMEM(block, bf16),
            pltpu.VMEM((frames + 2 * BAND, pos, width), bf16),
            pltpu.VMEM((frames + 2 * BAND, pos, width), bf16),
            pltpu.VMEM((8, 128), bf16),
            pltpu.VMEM(text_table.shape, bf16),
            pltpu.VMEM(text_proj.shape, bf16),
            pltpu.VMEM(w_query.shape, bf16),
            pltpu.VMEM(w_key.shape, bf16),
            pltpu.VMEM(w_value.shape, bf16),
            pltpu.VMEM(w_out.shape, bf16),
            pltpu.VMEM((n, 1, text_table.shape[1]), f32),
            pltpu.VMEM((n, 1, 128), f32),
            pltpu.VMEM((frames, 1, width), f32),
            pltpu.VMEM((frames, 1, width), f32),
            pltpu.VMEM((SPAN, frames, 1, 128), f32),
            pltpu.VMEM((width, 128), bf16),
            pltpu.VMEM((128, width), bf16),
            dma((n,)),
            dma((n,)),
            dma((n,)),
            dma((n,)),
            dma((n,)),
            dma((n,)),
            dma((n,)),
            dma((n,)),
            dma((9,)),
        ],
        compiler_params=pltpu.CompilerParams(
            collective_id=0, has_side_effects=True, vmem_limit_bytes=60 << 20
        ),
        name="queue",
    )(
        latents.reshape(fdev, n, pos, width),
        meta,
        text_ids[:, None],
        text_table,
        text_proj,
        level_embed,
        srate,
        norm_gain[None, :],
        w_query,
        w_key,
        w_value,
        w_out,
    )
    return out.reshape(fdev, tokens, width)


def general(
    latents,
    levels,
    back_reach,
    text_ids,
    text_table,
    text_proj,
    level_embed,
    step_rate,
    norm_gain,
    w_query,
    w_key,
    w_value,
    w_out,
):
    n = lax.axis_size("level")
    index = lax.axis_index("level")
    fdev, tokens, width = latents.shape
    heads = width // DH
    frames = fdev * n
    vocab = text_table.shape[0]
    spots = index * vocab + jnp.arange(vocab, dtype=jnp.int32)
    counts = jnp.sum((text_ids[:, None] == spots[None, :]).astype(jnp.float32), axis=0)
    partial = jnp.dot(
        counts.astype(jnp.bfloat16)[None, :], text_table, preferred_element_type=jnp.float32
    )
    pooled = lax.psum(partial, "level") / text_ids.shape[0]
    text_vec = jnp.dot(pooled.astype(jnp.bfloat16), text_proj, preferred_element_type=jnp.float32)
    levels = lax.all_gather(levels, "level", tiled=True)
    reach = lax.all_gather(back_reach, "level", tiled=True)
    cond = level_embed[levels] + text_vec
    rate = step_rate[levels]
    current = lax.all_to_all(latents, "level", split_axis=1, concat_axis=0, tiled=True)
    pos = tokens // n
    spot = jnp.arange(frames, dtype=jnp.int32)
    for step in range(STEPS):
        hin = current.astype(jnp.float32) + cond[:, None, :]
        power = jnp.mean(hin * hin, axis=-1, keepdims=True)
        normed = (hin * lax.rsqrt(power + 1e-06) * norm_gain).astype(jnp.bfloat16)
        flat = normed.reshape(-1, width)

        def project(weight):
            out = jnp.dot(flat, weight, preferred_element_type=jnp.float32)
            return out.astype(jnp.bfloat16).reshape(frames, pos, heads, DH).astype(jnp.float32)

        edge = ((BAND, BAND), (0, 0), (0, 0), (0, 0))
        query = project(w_query)
        keys = jnp.pad(project(w_key), edge)
        values = jnp.pad(project(w_value), edge)
        scores = []
        masks = []
        for offset in range(-BAND, BAND + 1):
            raw = jnp.sum(query * keys[BAND + offset : BAND + offset + frames], -1) / DH**0.5
            valid = (offset >= -reach) & (spot + offset >= 0) & (spot + offset < frames)
            scores.append(jnp.where(valid[:, None, None], raw, -1e30))
            masks.append(valid.astype(jnp.float32)[:, None, None])
        scores = jnp.stack(scores)
        expo = jnp.exp(scores - jnp.max(scores, axis=0)[None]) * jnp.stack(masks)
        weights = (expo / jnp.sum(expo, axis=0)[None]).astype(jnp.bfloat16).astype(jnp.float32)
        attended = jnp.zeros((frames, pos, heads, DH), jnp.float32)
        for slot in range(SPAN):
            attended = attended + weights[slot][..., None] * values[slot : slot + frames]
        noise = jnp.dot(
            attended.astype(jnp.bfloat16).reshape(-1, width),
            w_out,
            preferred_element_type=jnp.float32,
        ).reshape(frames, pos, width)
        updated = current.astype(jnp.float32) - rate[:, None, None] * noise
        current = jnp.roll(updated.astype(jnp.bfloat16), fdev, axis=0)
    return lax.all_to_all(current, "level", split_axis=0, concat_axis=1, tiled=True)


def per_device(latents, *rest):
    n = lax.axis_size("level")
    tokens = latents.shape[1]
    if tokens % (16 * n) == 0:
        return fused(latents, *rest)
    return general(latents, *rest)


def solution(mesh):
    in_specs = (
        P(("groups", "level"), None, None),
        P(("groups", "level")),
        P(("groups", "level")),
        P("groups"),
        P("level", None),
        P(),
        P(),
        P(),
        P(),
        P(),
        P(),
        P(),
        P(),
    )
    out_specs = P(("groups", "level"), None, None)
    return jax.shard_map(
        per_device, mesh=mesh, in_specs=in_specs, out_specs=out_specs, check_vma=False
    )
```

```python
import functools

import jax
import jax.numpy as jnp
from jax import lax
from jax.experimental import pallas as pl
from jax.experimental.pallas import tpu as pltpu
from jax.sharding import PartitionSpec as P

DH = 64
BAND = 2
STEPS = 3
SPAN = 2 * BAND + 1
MESH = pl.DeviceIdType.MESH


def queue_kernel(
    n,
    blocks,
    x_hbm,
    level_hbm,
    reach_hbm,
    ids_hbm,
    table_hbm,
    proj_hbm,
    embed_hbm,
    srate_hbm,
    gain_hbm,
    wq_hbm,
    wk_hbm,
    wv_hbm,
    wo_hbm,
    out_hbm,
    recv,
    xa,
    xb,
    xo,
    q_s,
    k_even,
    k_odd,
    v_even,
    v_odd,
    table,
    proj,
    embed,
    gain_s,
    wq,
    wk,
    wv,
    wo,
    level_s,
    reach_s,
    ids_s,
    srate_s,
    pool,
    metas,
    cond,
    rate,
    mask,
    fold,
    unfold,
    x_send,
    x_recv,
    p_send,
    p_recv,
    m_send,
    m_recv,
    o_send,
    o_recv,
    local,
):
    me = lax.axis_index("level")
    fdev = x_hbm.shape[0]
    halves, frames, pos, width = recv.shape
    rows = frames * pos
    pad = BAND * pos
    barrier = pltpu.get_barrier_semaphore()
    for hop in range(1, n):
        pl.semaphore_signal(
            barrier, inc=1, device_id={"level": lax.rem(me + hop, n)}, device_id_type=MESH
        )
    mine = pl.ds(me * fdev, fdev)
    pairs = [
        (level_hbm, level_s),
        (reach_hbm, reach_s),
        (ids_hbm, ids_s),
        (srate_hbm, srate_s),
        (table_hbm, table),
        (embed_hbm, embed),
        (gain_hbm, gain_s),
        (proj_hbm, proj),
        (wq_hbm, wq),
        (wk_hbm, wk),
        (wv_hbm, wv),
        (wo_hbm, wo),
    ] + [(x_hbm.at[:, me, h], recv.at[h, mine]) for h in range(halves)]
    stage = [
        pltpu.make_async_copy(src, dst, local.at[slot]) for slot, (src, dst) in enumerate(pairs)
    ]
    for copy in stage:
        copy.start()

    def x_copy(h, peer, owner):
        return pltpu.make_async_remote_copy(
            src_ref=x_hbm.at[:, peer, h],
            dst_ref=recv.at[h, pl.ds(owner * fdev, fdev)],
            send_sem=x_send.at[h, peer],
            recv_sem=x_recv.at[h, owner],
            device_id={"level": peer},
            device_id_type=MESH,
        )

    def p_copy(peer, owner):
        return pltpu.make_async_remote_copy(
            src_ref=pool.at[owner],
            dst_ref=pool.at[owner],
            send_sem=p_send.at[peer],
            recv_sem=p_recv.at[owner],
            device_id={"level": peer},
            device_id_type=MESH,
        )

    def m_copy(peer, owner):
        return pltpu.make_async_remote_copy(
            src_ref=metas.at[owner],
            dst_ref=metas.at[owner],
            send_sem=m_send.at[peer],
            recv_sem=m_recv.at[owner],
            device_id={"level": peer},
            device_id_type=MESH,
        )

    def o_copy(h, section, owner, peer):
        return pltpu.make_async_remote_copy(
            src_ref=xo.at[h, pl.ds(section * fdev, fdev)],
            dst_ref=out_hbm.at[:, owner, h],
            send_sem=o_send.at[h, peer],
            recv_sem=o_recv.at[h, owner],
            device_id={"level": peer},
            device_id_type=MESH,
        )

    peers = [lax.rem(me + hop, n) for hop in range(1, n)]
    pl.semaphore_wait(barrier, n - 1)
    for peer in peers:
        x_copy(0, peer, me).start()

    stage[0].wait()
    stage[1].wait()
    lane = lax.broadcasted_iota(jnp.int32, (1, 128), 1)
    fact = jnp.zeros((1, 128), jnp.int32)
    for f in range(fdev):
        fact = jnp.where(lane == f, level_s[f], fact)
        fact = jnp.where(lane == fdev + f, reach_s[f], fact)
    metas[me] = fact
    for peer in peers:
        m_copy(peer, me).start()

    vocab = table.shape[0]
    stage[2].wait()
    first_id = me * vocab
    spots = lax.broadcasted_iota(jnp.int32, (1, vocab), 1) + first_id
    counts = jnp.zeros((1, vocab), jnp.float32)
    text_tokens = ids_s.shape[0]
    for token in range(text_tokens):
        counts = counts + jnp.where(spots == ids_s[token], 1.0, 0.0)
    counts = jnp.broadcast_to(counts, (16, vocab)).astype(jnp.bfloat16)
    stage[4].wait()
    partial = jnp.dot(counts, table[...], preferred_element_type=jnp.float32)
    pool[me] = partial[0:1]
    for peer in peers:
        p_copy(peer, me).start()
    for h in range(1, halves):
        for peer in peers:
            x_copy(h, peer, me).start()

    row = lax.broadcasted_iota(jnp.int32, (width, 128), 0)
    col = lax.broadcasted_iota(jnp.int32, (width, 128), 1) * DH
    fold[...] = ((row >= col) & (row < col + DH)).astype(jnp.float32).astype(jnp.bfloat16)
    row = lax.broadcasted_iota(jnp.int32, (128, width), 0) * DH
    col = lax.broadcasted_iota(jnp.int32, (128, width), 1)
    unfold[...] = ((col >= row) & (col < row + DH)).astype(jnp.float32).astype(jnp.bfloat16)
    edge = jnp.zeros((pad, width), jnp.bfloat16)
    for buffer in (k_even, v_even):
        buffer[0:pad] = edge
        buffer[rows + pad : rows + 2 * pad] = edge

    for slot in (3, 5, 6, 7):
        stage[slot].wait()
    for peer in peers:
        m_copy(peer, peer).wait_recv()
    facts = metas[...].reshape(n, 128)
    slot_index = lax.broadcasted_iota(jnp.int32, (n, 128), 0)
    bases = []
    for f in range(fdev):
        level = facts[:, f : f + 1]
        base = jnp.zeros((n, width), jnp.float32)
        speed = jnp.zeros((n, width), jnp.float32)
        for number in range(embed.shape[0]):
            chosen = level == number
            base = base + jnp.where(chosen, embed[number : number + 1, :], 0.0)
            speed = speed + jnp.where(chosen, srate_s[number], 0.0)
        bases.append(base)
        reach = jnp.broadcast_to(facts[:, fdev + f : fdev + f + 1], (n, 128))
        spot = slot_index * fdev + f
        for s in range(n):
            rate[s * fdev + f] = speed[s : s + 1]
        for slot in range(SPAN):
            offset = slot - BAND
            valid = ((reach >= -offset) & (spot + offset >= 0) & (spot + offset < frames)).astype(
                jnp.float32
            )
            for s in range(n):
                mask[slot, s * fdev + f] = valid[s : s + 1]

    for peer in peers:
        p_copy(peer, peer).wait_recv()
    pooled = jnp.sum(pool[...], axis=0) / float(text_tokens)
    pooled = jnp.broadcast_to(pooled, (16, pooled.shape[1])).astype(jnp.bfloat16)
    text = jnp.dot(pooled, proj[...], preferred_element_type=jnp.float32)[0:1]
    for f in range(fdev):
        full = bases[f] + text
        for s in range(n):
            cond[s * fdev + f] = full[s : s + 1]

    for slot in (8, 9, 10, 11):
        stage[slot].wait()

    gain = gain_s[...].reshape(1, 1, width)
    scale = 1.0 / DH**0.5
    group = frames // blocks
    size = group * pos

    def project(current):
        hin = current + cond[...]
        power = jnp.mean(hin * hin, axis=-1, keepdims=True)
        flat = (hin * lax.rsqrt(power + 1e-06) * gain).reshape(rows, width).astype(jnp.bfloat16)
        q_s[...] = jnp.dot(flat, wq[...], preferred_element_type=jnp.float32).astype(jnp.bfloat16)
        fill = jnp.zeros((pos, width), jnp.float32)
        for weight, even, odd in ((wk, k_even, k_odd), (wv, v_even, v_odd)):
            made = jnp.dot(flat, weight[...], preferred_element_type=jnp.float32)
            even[pad : pad + rows] = made.astype(jnp.bfloat16)
            odd[0 : rows + 2 * pos] = jnp.concatenate([fill, made, fill], axis=0).astype(
                jnp.bfloat16
            )

    def attend(first, current):
        at = pl.ds(first, group)
        start = first * pos

        def shifted(even, odd, slot):
            source = even if slot % 2 == 0 else odd
            return source[pl.ds(pl.multiple_of(start + (slot - slot % 2) * pos, 16), size)]

        query = q_s[pl.ds(pl.multiple_of(start, 16), size)]
        scores = []
        masks = []
        for slot in range(SPAN):
            keys = shifted(k_even, k_odd, slot)
            raw = jnp.dot(query * keys, fold[...], preferred_element_type=jnp.float32) * scale
            valid = mask[slot, at]
            scores.append(jnp.where(valid > 0.0, raw.reshape(group, pos, 128), -1e30))
            masks.append(valid)
        top = functools.reduce(jnp.maximum, scores)
        expo = [jnp.exp(score - top) * valid for score, valid in zip(scores, masks)]
        inverse = 1.0 / functools.reduce(jnp.add, expo)
        total = None
        for slot in range(SPAN):
            weight = (expo[slot] * inverse).reshape(size, 128).astype(jnp.bfloat16)
            spread = jnp.dot(weight, unfold[...], preferred_element_type=jnp.float32)
            term = spread * shifted(v_even, v_odd, slot).astype(jnp.float32)
            total = term if total is None else total + term
        noise = jnp.dot(total.astype(jnp.bfloat16), wo[...], preferred_element_type=jnp.float32)
        return current - rate[at] * noise.reshape(group, pos, width)

    def half(h, carry):
        stage_x = pltpu.make_async_copy(x_hbm.at[:, me, h], recv.at[h, mine], local.at[12 + h])
        stage_x.wait()
        for peer in peers:
            x_copy(h, peer, peer).wait_recv()
        turn = fdev * pos
        for step in range(STEPS):
            last = step == STEPS - 1
            held = xa if step % 2 == 1 else xb
            fresh = xb if step % 2 == 1 else xa

            def load(first, count, step=step, held=held):
                if step == 0:
                    return recv[h, pl.ds(first, count)].astype(jnp.float32)
                start = pl.multiple_of(first * pos, 16)
                return (
                    held[pl.ds(start, count * pos)].astype(jnp.float32).reshape(count, pos, width)
                )

            project(load(0, frames))

            def body(index, carry, load=load, fresh=fresh, last=last):
                first = index * group
                made = attend(first, load(first, group))
                if last:
                    xo[h, pl.ds(first, group)] = made.astype(jnp.bfloat16)
                else:
                    spot = pl.multiple_of(first * pos + turn, 16)
                    fresh[pl.ds(spot, size)] = made.reshape(size, width).astype(jnp.bfloat16)
                return carry

            lax.fori_loop(0, blocks, body, 0)
            if not last:
                fresh[0:turn] = fresh[rows : rows + turn]
        for peer in peers:
            o_copy(h, lax.rem(peer + n - 1, n), me, peer).start()
        pltpu.make_async_copy(
            xo.at[h, pl.ds(lax.rem(me + n - 1, n) * fdev, fdev)],
            out_hbm.at[:, me, h],
            local.at[12 + halves + h],
        ).start()
        return carry

    lax.fori_loop(0, halves, half, 0)

    for h in range(halves):
        for peer in peers:
            x_copy(h, peer, me).wait_send()
    for peer in peers:
        m_copy(peer, me).wait_send()
        p_copy(peer, me).wait_send()
    for h in range(halves):
        pltpu.make_async_copy(
            xo.at[h, pl.ds(lax.rem(me + n - 1, n) * fdev, fdev)],
            out_hbm.at[:, me, h],
            local.at[12 + halves + h],
        ).wait()
        for peer in peers:
            o_copy(h, lax.rem(peer + n - 1, n), me, peer).wait_send()
            o_copy(h, lax.rem(me + n - 1, n), peer, me).wait_recv()


HALVES = 2
BLOCKS = 1
GRANT = 40 << 20


def fused(
    latents,
    levels,
    back_reach,
    text_ids,
    text_table,
    text_proj,
    level_embed,
    step_rate,
    norm_gain,
    w_query,
    w_key,
    w_value,
    w_out,
):
    n = lax.axis_size("level")
    fdev, tokens, width = latents.shape
    pos = tokens // (n * HALVES)
    frames = fdev * n
    rows = frames * pos
    bf16, f32, i32 = jnp.bfloat16, jnp.float32, jnp.int32
    anywhere = pl.BlockSpec(memory_space=pl.ANY)
    stored = pl.BlockSpec(memory_space=pltpu.HBM)
    dma = pltpu.SemaphoreType.DMA
    block = pltpu.VMEM((HALVES, frames, pos, width), bf16)
    rolled = pltpu.VMEM((rows + fdev * pos, width), bf16)
    padded = pltpu.VMEM((rows + 2 * BAND * pos, width), bf16)
    square = pltpu.VMEM((width, width), bf16)
    out = pl.pallas_call(
        functools.partial(queue_kernel, n, BLOCKS),
        out_shape=jax.ShapeDtypeStruct((fdev, n, HALVES, pos, width), bf16),
        in_specs=[stored] * 13,
        out_specs=anywhere,
        scratch_shapes=[
            block,
            rolled,
            rolled,
            block,
            pltpu.VMEM((rows, width), bf16),
            padded,
            padded,
            padded,
            padded,
            pltpu.VMEM(text_table.shape, bf16),
            pltpu.VMEM(text_proj.shape, bf16),
            pltpu.VMEM(level_embed.shape, f32),
            pltpu.VMEM(norm_gain.shape, f32),
            square,
            square,
            square,
            square,
            pltpu.SMEM(levels.shape, i32),
            pltpu.SMEM(back_reach.shape, i32),
            pltpu.SMEM(text_ids.shape, i32),
            pltpu.SMEM(step_rate.shape, f32),
            pltpu.VMEM((n, 1, text_table.shape[1]), f32),
            pltpu.VMEM((n, 1, 128), i32),
            pltpu.VMEM((frames, 1, width), f32),
            pltpu.VMEM((frames, 1, width), f32),
            pltpu.VMEM((SPAN, frames, 1, 128), f32),
            pltpu.VMEM((width, 128), bf16),
            pltpu.VMEM((128, width), bf16),
            dma((HALVES, n)),
            dma((HALVES, n)),
            dma((n,)),
            dma((n,)),
            dma((n,)),
            dma((n,)),
            dma((HALVES, n)),
            dma((HALVES, n)),
            dma((12 + 2 * HALVES,)),
        ],
        compiler_params=pltpu.CompilerParams(
            collective_id=0, has_side_effects=True, vmem_limit_bytes=GRANT
        ),
        name="queue",
    )(
        *(
            pltpu.with_memory_space_constraint(value, pltpu.HBM)
            for value in (
                latents.reshape(fdev, n, HALVES, pos, width),
                levels,
                back_reach,
                text_ids,
                text_table,
                text_proj,
                level_embed,
                step_rate,
                norm_gain,
                w_query,
                w_key,
                w_value,
                w_out,
            )
        )
    )
    return out.reshape(fdev, tokens, width)


def general(
    latents,
    levels,
    back_reach,
    text_ids,
    text_table,
    text_proj,
    level_embed,
    step_rate,
    norm_gain,
    w_query,
    w_key,
    w_value,
    w_out,
):
    n = lax.axis_size("level")
    index = lax.axis_index("level")
    fdev, tokens, width = latents.shape
    heads = width // DH
    frames = fdev * n
    vocab = text_table.shape[0]
    spots = index * vocab + jnp.arange(vocab, dtype=jnp.int32)
    counts = jnp.sum((text_ids[:, None] == spots[None, :]).astype(jnp.float32), axis=0)
    partial = jnp.dot(
        counts.astype(jnp.bfloat16)[None, :], text_table, preferred_element_type=jnp.float32
    )
    pooled = lax.psum(partial, "level") / text_ids.shape[0]
    text_vec = jnp.dot(pooled.astype(jnp.bfloat16), text_proj, preferred_element_type=jnp.float32)
    levels = lax.all_gather(levels, "level", tiled=True)
    reach = lax.all_gather(back_reach, "level", tiled=True)
    cond = level_embed[levels] + text_vec
    rate = step_rate[levels]
    current = lax.all_to_all(latents, "level", split_axis=1, concat_axis=0, tiled=True)
    pos = tokens // n
    spot = jnp.arange(frames, dtype=jnp.int32)
    for step in range(STEPS):
        hin = current.astype(jnp.float32) + cond[:, None, :]
        power = jnp.mean(hin * hin, axis=-1, keepdims=True)
        normed = (hin * lax.rsqrt(power + 1e-06) * norm_gain).astype(jnp.bfloat16)
        flat = normed.reshape(-1, width)

        def project(weight):
            out = jnp.dot(flat, weight, preferred_element_type=jnp.float32)
            return out.astype(jnp.bfloat16).reshape(frames, pos, heads, DH).astype(jnp.float32)

        edge = ((BAND, BAND), (0, 0), (0, 0), (0, 0))
        query = project(w_query)
        keys = jnp.pad(project(w_key), edge)
        values = jnp.pad(project(w_value), edge)
        scores = []
        masks = []
        for offset in range(-BAND, BAND + 1):
            raw = jnp.sum(query * keys[BAND + offset : BAND + offset + frames], -1) / DH**0.5
            valid = (offset >= -reach) & (spot + offset >= 0) & (spot + offset < frames)
            scores.append(jnp.where(valid[:, None, None], raw, -1e30))
            masks.append(valid.astype(jnp.float32)[:, None, None])
        scores = jnp.stack(scores)
        expo = jnp.exp(scores - jnp.max(scores, axis=0)[None]) * jnp.stack(masks)
        weights = (expo / jnp.sum(expo, axis=0)[None]).astype(jnp.bfloat16).astype(jnp.float32)
        attended = jnp.zeros((frames, pos, heads, DH), jnp.float32)
        for slot in range(SPAN):
            attended = attended + weights[slot][..., None] * values[slot : slot + frames]
        noise = jnp.dot(
            attended.astype(jnp.bfloat16).reshape(-1, width),
            w_out,
            preferred_element_type=jnp.float32,
        ).reshape(frames, pos, width)
        updated = current.astype(jnp.float32) - rate[:, None, None] * noise
        current = jnp.roll(updated.astype(jnp.bfloat16), fdev, axis=0)
    return lax.all_to_all(current, "level", split_axis=0, concat_axis=1, tiled=True)


def per_device(latents, *rest):
    n = lax.axis_size("level")
    tokens = latents.shape[1]
    if tokens % (8 * HALVES * n) == 0 and latents.shape[0] % 2 == 0:
        return fused(latents, *rest)
    return general(latents, *rest)


def solution(mesh):
    in_specs = (
        P(("groups", "level"), None, None),
        P(("groups", "level")),
        P(("groups", "level")),
        P("groups"),
        P("level", None),
        P(),
        P(),
        P(),
        P(),
        P(),
        P(),
        P(),
        P(),
    )
    out_specs = P(("groups", "level"), None, None)
    return jax.shard_map(
        per_device, mesh=mesh, in_specs=in_specs, out_specs=out_specs, check_vma=False
    )
```

```python
import functools

import jax
import jax.numpy as jnp
from jax import lax
from jax.experimental import pallas as pl
from jax.experimental.pallas import tpu as pltpu
from jax.sharding import PartitionSpec as P

DH = 64
BAND = 2
STEPS = 3
SPAN = 2 * BAND + 1
MESH = pl.DeviceIdType.MESH


def queue_kernel(
    n,
    blocks,
    x_hbm,
    level_hbm,
    reach_hbm,
    ids_hbm,
    table_hbm,
    proj_hbm,
    embed_hbm,
    srate_hbm,
    gain_hbm,
    wq_hbm,
    wk_hbm,
    wv_hbm,
    wo_hbm,
    out_hbm,
    recv,
    xa,
    xb,
    xo,
    q_s,
    k_even,
    k_odd,
    v_even,
    v_odd,
    table,
    proj,
    embed,
    gain_s,
    wq,
    wk,
    wv,
    wo,
    level_s,
    reach_s,
    ids_s,
    srate_s,
    pool,
    metas,
    cond,
    rate,
    mask,
    fold,
    unfold,
    x_send,
    x_recv,
    p_send,
    p_recv,
    m_send,
    m_recv,
    o_send,
    o_recv,
    local,
):
    me = lax.axis_index("level")
    fdev = x_hbm.shape[0]
    halves, frames, pos, width = recv.shape
    rows = frames * pos
    pad = BAND * pos
    barrier = pltpu.get_barrier_semaphore()
    for hop in range(1, n):
        pl.semaphore_signal(
            barrier, inc=1, device_id={"level": lax.rem(me + hop, n)}, device_id_type=MESH
        )
    mine = pl.ds(me * fdev, fdev)
    pairs = [
        (level_hbm, level_s),
        (reach_hbm, reach_s),
        (ids_hbm, ids_s),
        (srate_hbm, srate_s),
        (table_hbm, table),
        (embed_hbm, embed),
        (gain_hbm, gain_s),
        (proj_hbm, proj),
        (wq_hbm, wq),
        (wk_hbm, wk),
        (wv_hbm, wv),
        (wo_hbm, wo),
    ] + [(x_hbm.at[:, me, h], recv.at[h, mine]) for h in range(halves)]
    stage = [
        pltpu.make_async_copy(src, dst, local.at[slot]) for slot, (src, dst) in enumerate(pairs)
    ]
    for copy in stage:
        copy.start()

    def x_copy(h, peer, owner):
        return pltpu.make_async_remote_copy(
            src_ref=x_hbm.at[:, peer, h],
            dst_ref=recv.at[h, pl.ds(owner * fdev, fdev)],
            send_sem=x_send.at[h, peer],
            recv_sem=x_recv.at[h, owner],
            device_id={"level": peer},
            device_id_type=MESH,
        )

    def p_copy(peer, owner):
        return pltpu.make_async_remote_copy(
            src_ref=pool.at[owner],
            dst_ref=pool.at[owner],
            send_sem=p_send.at[peer],
            recv_sem=p_recv.at[owner],
            device_id={"level": peer},
            device_id_type=MESH,
        )

    def m_copy(peer, owner):
        return pltpu.make_async_remote_copy(
            src_ref=metas.at[owner],
            dst_ref=metas.at[owner],
            send_sem=m_send.at[peer],
            recv_sem=m_recv.at[owner],
            device_id={"level": peer},
            device_id_type=MESH,
        )

    def o_copy(h, section, owner, peer):
        return pltpu.make_async_remote_copy(
            src_ref=xo.at[h, pl.ds(section * fdev, fdev)],
            dst_ref=out_hbm.at[:, owner, h],
            send_sem=o_send.at[h, peer],
            recv_sem=o_recv.at[h, owner],
            device_id={"level": peer},
            device_id_type=MESH,
        )

    order = sorted(range(1, n), key=lambda hop: min(hop, n - hop))
    peers = [lax.rem(me + hop, n) for hop in order]
    pl.semaphore_wait(barrier, n - 1)
    early = (n - 1) * 9 // 15
    for peer in peers[:early]:
        x_copy(0, peer, me).start()

    stage[0].wait()
    stage[1].wait()
    lane = lax.broadcasted_iota(jnp.int32, (1, 128), 1)
    fact = jnp.zeros((1, 128), jnp.int32)
    for f in range(fdev):
        fact = jnp.where(lane == f, level_s[f], fact)
        fact = jnp.where(lane == fdev + f, reach_s[f], fact)
    metas[me] = fact
    for peer in peers:
        m_copy(peer, me).start()

    vocab = table.shape[0]
    stage[2].wait()
    first_id = me * vocab
    spots = lax.broadcasted_iota(jnp.int32, (1, vocab), 1) + first_id
    counts = jnp.zeros((1, vocab), jnp.float32)
    text_tokens = ids_s.shape[0]
    for token in range(text_tokens):
        counts = counts + jnp.where(spots == ids_s[token], 1.0, 0.0)
    counts = jnp.broadcast_to(counts, (16, vocab)).astype(jnp.bfloat16)
    stage[4].wait()
    partial = jnp.dot(counts, table[...], preferred_element_type=jnp.float32)
    pool[me] = partial[0:1]
    for peer in peers:
        p_copy(peer, me).start()
    for peer in peers[early:]:
        x_copy(0, peer, me).start()
    for h in range(1, halves):
        for peer in peers:
            x_copy(h, peer, me).start()

    row = lax.broadcasted_iota(jnp.int32, (width, 128), 0)
    col = lax.broadcasted_iota(jnp.int32, (width, 128), 1) * DH
    fold[...] = ((row >= col) & (row < col + DH)).astype(jnp.float32).astype(jnp.bfloat16)
    row = lax.broadcasted_iota(jnp.int32, (128, width), 0) * DH
    col = lax.broadcasted_iota(jnp.int32, (128, width), 1)
    unfold[...] = ((col >= row) & (col < row + DH)).astype(jnp.float32).astype(jnp.bfloat16)
    edge = jnp.zeros((pad, width), jnp.bfloat16)
    for buffer in (k_even, v_even):
        buffer[0:pad] = edge
        buffer[rows + pad : rows + 2 * pad] = edge

    for slot in (3, 5, 6, 7):
        stage[slot].wait()
    for peer in peers:
        m_copy(peer, peer).wait_recv()
    facts = metas[...].reshape(n, 128)
    slot_index = lax.broadcasted_iota(jnp.int32, (n, 128), 0)
    bases = []
    for f in range(fdev):
        level = facts[:, f : f + 1]
        base = jnp.zeros((n, width), jnp.float32)
        speed = jnp.zeros((n, width), jnp.float32)
        for number in range(embed.shape[0]):
            chosen = level == number
            base = base + jnp.where(chosen, embed[number : number + 1, :], 0.0)
            speed = speed + jnp.where(chosen, srate_s[number], 0.0)
        bases.append(base)
        reach = jnp.broadcast_to(facts[:, fdev + f : fdev + f + 1], (n, 128))
        spot = slot_index * fdev + f
        for s in range(n):
            rate[s * fdev + f] = speed[s : s + 1]
        for slot in range(SPAN):
            offset = slot - BAND
            valid = ((reach >= -offset) & (spot + offset >= 0) & (spot + offset < frames)).astype(
                jnp.float32
            )
            for s in range(n):
                mask[slot, s * fdev + f] = valid[s : s + 1]

    for peer in peers:
        p_copy(peer, peer).wait_recv()
    pooled = jnp.sum(pool[...], axis=0) / float(text_tokens)
    pooled = jnp.broadcast_to(pooled, (16, pooled.shape[1])).astype(jnp.bfloat16)
    text = jnp.dot(pooled, proj[...], preferred_element_type=jnp.float32)[0:1]
    for f in range(fdev):
        full = bases[f] + text
        for s in range(n):
            cond[s * fdev + f] = full[s : s + 1]

    for slot in (8, 9, 10, 11):
        stage[slot].wait()

    gain = gain_s[...].reshape(1, 1, width)
    scale = 1.0 / DH**0.5
    group = frames // blocks
    size = group * pos

    def project(current):
        hin = current + cond[...]
        power = jnp.mean(hin * hin, axis=-1, keepdims=True)
        flat = (hin * lax.rsqrt(power + 1e-06) * gain).reshape(rows, width).astype(jnp.bfloat16)
        q_s[...] = jnp.dot(flat, wq[...], preferred_element_type=jnp.float32).astype(jnp.bfloat16)
        fill = jnp.zeros((pos, width), jnp.float32)
        for weight, even, odd in ((wk, k_even, k_odd), (wv, v_even, v_odd)):
            made = jnp.dot(flat, weight[...], preferred_element_type=jnp.float32)
            even[pad : pad + rows] = made.astype(jnp.bfloat16)
            odd[0 : rows + 2 * pos] = jnp.concatenate([fill, made, fill], axis=0).astype(
                jnp.bfloat16
            )

    def attend(first, current):
        at = pl.ds(first, group)
        start = first * pos

        def shifted(even, odd, slot):
            source = even if slot % 2 == 0 else odd
            return source[pl.ds(pl.multiple_of(start + (slot - slot % 2) * pos, 16), size)]

        query = q_s[pl.ds(pl.multiple_of(start, 16), size)]
        scores = []
        masks = []
        for slot in range(SPAN):
            keys = shifted(k_even, k_odd, slot)
            raw = jnp.dot(query * keys, fold[...], preferred_element_type=jnp.float32) * scale
            valid = mask[slot, at]
            scores.append(jnp.where(valid > 0.0, raw.reshape(group, pos, 128), -1e30))
            masks.append(valid)
        top = functools.reduce(jnp.maximum, scores)
        expo = [jnp.exp(score - top) * valid for score, valid in zip(scores, masks)]
        inverse = 1.0 / functools.reduce(jnp.add, expo)
        total = None
        for slot in range(SPAN):
            weight = (expo[slot] * inverse).reshape(size, 128).astype(jnp.bfloat16)
            spread = jnp.dot(weight, unfold[...], preferred_element_type=jnp.float32)
            term = spread * shifted(v_even, v_odd, slot).astype(jnp.float32)
            total = term if total is None else total + term
        noise = jnp.dot(total.astype(jnp.bfloat16), wo[...], preferred_element_type=jnp.float32)
        return current - rate[at] * noise.reshape(group, pos, width)

    def half(h, carry):
        stage_x = pltpu.make_async_copy(x_hbm.at[:, me, h], recv.at[h, mine], local.at[12 + h])
        stage_x.wait()
        for peer in peers:
            x_copy(h, peer, peer).wait_recv()
        turn = fdev * pos
        for step in range(STEPS):
            last = step == STEPS - 1
            held = xa if step % 2 == 1 else xb
            fresh = xb if step % 2 == 1 else xa

            def load(first, count, step=step, held=held):
                if step == 0:
                    return recv[h, pl.ds(first, count)].astype(jnp.float32)
                start = pl.multiple_of(first * pos, 16)
                return (
                    held[pl.ds(start, count * pos)].astype(jnp.float32).reshape(count, pos, width)
                )

            project(load(0, frames))

            def body(index, carry, load=load, fresh=fresh, last=last):
                first = index * group
                made = attend(first, load(first, group))
                if last:
                    xo[h, pl.ds(first, group)] = made.astype(jnp.bfloat16)
                else:
                    spot = pl.multiple_of(first * pos + turn, 16)
                    fresh[pl.ds(spot, size)] = made.reshape(size, width).astype(jnp.bfloat16)
                return carry

            lax.fori_loop(0, blocks, body, 0)
            if not last:
                fresh[0:turn] = fresh[rows : rows + turn]
        for peer in peers:
            o_copy(h, lax.rem(peer + n - 1, n), me, peer).start()
        pltpu.make_async_copy(
            xo.at[h, pl.ds(lax.rem(me + n - 1, n) * fdev, fdev)],
            out_hbm.at[:, me, h],
            local.at[12 + halves + h],
        ).start()
        return carry

    lax.fori_loop(0, halves, half, 0)

    for h in range(halves):
        for peer in peers:
            x_copy(h, peer, me).wait_send()
    for peer in peers:
        m_copy(peer, me).wait_send()
        p_copy(peer, me).wait_send()
    for h in range(halves):
        pltpu.make_async_copy(
            xo.at[h, pl.ds(lax.rem(me + n - 1, n) * fdev, fdev)],
            out_hbm.at[:, me, h],
            local.at[12 + halves + h],
        ).wait()
        for peer in peers:
            o_copy(h, lax.rem(peer + n - 1, n), me, peer).wait_send()
            o_copy(h, lax.rem(me + n - 1, n), peer, me).wait_recv()


HALVES = 2
BLOCKS = 1
GRANT = 40 << 20


def fused(
    latents,
    levels,
    back_reach,
    text_ids,
    text_table,
    text_proj,
    level_embed,
    step_rate,
    norm_gain,
    w_query,
    w_key,
    w_value,
    w_out,
):
    n = lax.axis_size("level")
    fdev, tokens, width = latents.shape
    pos = tokens // (n * HALVES)
    frames = fdev * n
    rows = frames * pos
    bf16, f32, i32 = jnp.bfloat16, jnp.float32, jnp.int32
    anywhere = pl.BlockSpec(memory_space=pl.ANY)
    stored = pl.BlockSpec(memory_space=pltpu.HBM)
    dma = pltpu.SemaphoreType.DMA
    block = pltpu.VMEM((HALVES, frames, pos, width), bf16)
    rolled = pltpu.VMEM((rows + fdev * pos, width), bf16)
    padded = pltpu.VMEM((rows + 2 * BAND * pos, width), bf16)
    square = pltpu.VMEM((width, width), bf16)
    out = pl.pallas_call(
        functools.partial(queue_kernel, n, BLOCKS),
        out_shape=jax.ShapeDtypeStruct((fdev, n, HALVES, pos, width), bf16),
        in_specs=[stored] * 13,
        out_specs=anywhere,
        scratch_shapes=[
            block,
            rolled,
            rolled,
            block,
            pltpu.VMEM((rows, width), bf16),
            padded,
            padded,
            padded,
            padded,
            pltpu.VMEM(text_table.shape, bf16),
            pltpu.VMEM(text_proj.shape, bf16),
            pltpu.VMEM(level_embed.shape, f32),
            pltpu.VMEM(norm_gain.shape, f32),
            square,
            square,
            square,
            square,
            pltpu.SMEM(levels.shape, i32),
            pltpu.SMEM(back_reach.shape, i32),
            pltpu.SMEM(text_ids.shape, i32),
            pltpu.SMEM(step_rate.shape, f32),
            pltpu.VMEM((n, 1, text_table.shape[1]), f32),
            pltpu.VMEM((n, 1, 128), i32),
            pltpu.VMEM((frames, 1, width), f32),
            pltpu.VMEM((frames, 1, width), f32),
            pltpu.VMEM((SPAN, frames, 1, 128), f32),
            pltpu.VMEM((width, 128), bf16),
            pltpu.VMEM((128, width), bf16),
            dma((HALVES, n)),
            dma((HALVES, n)),
            dma((n,)),
            dma((n,)),
            dma((n,)),
            dma((n,)),
            dma((HALVES, n)),
            dma((HALVES, n)),
            dma((12 + 2 * HALVES,)),
        ],
        compiler_params=pltpu.CompilerParams(
            collective_id=0, has_side_effects=True, vmem_limit_bytes=GRANT
        ),
        name="queue",
    )(
        *(
            pltpu.with_memory_space_constraint(value, pltpu.HBM)
            for value in (
                latents.reshape(fdev, n, HALVES, pos, width),
                levels,
                back_reach,
                text_ids,
                text_table,
                text_proj,
                level_embed,
                step_rate,
                norm_gain,
                w_query,
                w_key,
                w_value,
                w_out,
            )
        )
    )
    return out.reshape(fdev, tokens, width)


def general(
    latents,
    levels,
    back_reach,
    text_ids,
    text_table,
    text_proj,
    level_embed,
    step_rate,
    norm_gain,
    w_query,
    w_key,
    w_value,
    w_out,
):
    n = lax.axis_size("level")
    index = lax.axis_index("level")
    fdev, tokens, width = latents.shape
    heads = width // DH
    frames = fdev * n
    vocab = text_table.shape[0]
    spots = index * vocab + jnp.arange(vocab, dtype=jnp.int32)
    counts = jnp.sum((text_ids[:, None] == spots[None, :]).astype(jnp.float32), axis=0)
    partial = jnp.dot(
        counts.astype(jnp.bfloat16)[None, :], text_table, preferred_element_type=jnp.float32
    )
    pooled = lax.psum(partial, "level") / text_ids.shape[0]
    text_vec = jnp.dot(pooled.astype(jnp.bfloat16), text_proj, preferred_element_type=jnp.float32)
    levels = lax.all_gather(levels, "level", tiled=True)
    reach = lax.all_gather(back_reach, "level", tiled=True)
    cond = level_embed[levels] + text_vec
    rate = step_rate[levels]
    current = lax.all_to_all(latents, "level", split_axis=1, concat_axis=0, tiled=True)
    pos = tokens // n
    spot = jnp.arange(frames, dtype=jnp.int32)
    for step in range(STEPS):
        hin = current.astype(jnp.float32) + cond[:, None, :]
        power = jnp.mean(hin * hin, axis=-1, keepdims=True)
        normed = (hin * lax.rsqrt(power + 1e-06) * norm_gain).astype(jnp.bfloat16)
        flat = normed.reshape(-1, width)

        def project(weight):
            out = jnp.dot(flat, weight, preferred_element_type=jnp.float32)
            return out.astype(jnp.bfloat16).reshape(frames, pos, heads, DH).astype(jnp.float32)

        edge = ((BAND, BAND), (0, 0), (0, 0), (0, 0))
        query = project(w_query)
        keys = jnp.pad(project(w_key), edge)
        values = jnp.pad(project(w_value), edge)
        scores = []
        masks = []
        for offset in range(-BAND, BAND + 1):
            raw = jnp.sum(query * keys[BAND + offset : BAND + offset + frames], -1) / DH**0.5
            valid = (offset >= -reach) & (spot + offset >= 0) & (spot + offset < frames)
            scores.append(jnp.where(valid[:, None, None], raw, -1e30))
            masks.append(valid.astype(jnp.float32)[:, None, None])
        scores = jnp.stack(scores)
        expo = jnp.exp(scores - jnp.max(scores, axis=0)[None]) * jnp.stack(masks)
        weights = (expo / jnp.sum(expo, axis=0)[None]).astype(jnp.bfloat16).astype(jnp.float32)
        attended = jnp.zeros((frames, pos, heads, DH), jnp.float32)
        for slot in range(SPAN):
            attended = attended + weights[slot][..., None] * values[slot : slot + frames]
        noise = jnp.dot(
            attended.astype(jnp.bfloat16).reshape(-1, width),
            w_out,
            preferred_element_type=jnp.float32,
        ).reshape(frames, pos, width)
        updated = current.astype(jnp.float32) - rate[:, None, None] * noise
        current = jnp.roll(updated.astype(jnp.bfloat16), fdev, axis=0)
    return lax.all_to_all(current, "level", split_axis=0, concat_axis=1, tiled=True)


def per_device(latents, *rest):
    n = lax.axis_size("level")
    tokens = latents.shape[1]
    if tokens % (8 * HALVES * n) == 0 and latents.shape[0] % 2 == 0:
        return fused(latents, *rest)
    return general(latents, *rest)


def solution(mesh):
    in_specs = (
        P(("groups", "level"), None, None),
        P(("groups", "level")),
        P(("groups", "level")),
        P("groups"),
        P("level", None),
        P(),
        P(),
        P(),
        P(),
        P(),
        P(),
        P(),
        P(),
    )
    out_specs = P(("groups", "level"), None, None)
    return jax.shard_map(
        per_device, mesh=mesh, in_specs=in_specs, out_specs=out_specs, check_vma=False
    )
```
